128 devices in a mesh: dp: 16 (over y_lo, x, core), seq: 8 (over z, y_hi).
Axes of the slice: x: 4, y: 4 (y_hi: 2, y_lo: 2; y = y_hi * 2 + y_lo), z: 4, core: 2. Of those that a mesh axis runs over, the one named last changes fastest.
Arguments:
- query_input: bfloat16 [16, 1024, 2048], P('dp', 'seq'), may hold values from -6 to 6
- key_input: bfloat16 [16, 1024, 2048], P('dp', 'seq'), may hold values from -6 to 6
- value_input: bfloat16 [16, 1024, 2048], P('dp', 'seq'), may hold values from -6 to 6
- out_weight: bfloat16 [2048, 4096], P(None, 'dp'), may hold values from -0.125 to 0.125
- grad_out: bfloat16 [16, 1024, 4096], P('dp', 'seq'), may hold values from -6 to 6
Outputs:
- projected: bfloat16 [16, 1024, 4096], P('dp', 'seq')
- grad_query: bfloat16 [16, 1024, 2048], P('dp', None, 'seq')
- grad_key: bfloat16 [16, 1024, 2048], P('dp', None, 'seq')
- grad_value: bfloat16 [16, 1024, 2048], P('dp', None, 'seq')
- grad_weight: float32 [2048, 4096], P('seq', 'dp')
The draws below stay inside these ranges and needn't reach their ends.
All inputs are finite; a program needn't handle non-finite values.
Results may differ from the reference program's by a relative error of at most 0.022.
Values may be sent and summed in bfloat16 or wider, within the bound.
No kernel may reach another device: no remote copies, remote signals or barrier semaphores. Data moves between devices by JAX's collectives and lax.ppermute only.
A program may use at most 128 MiB of HBM per device.

```python
import jax
import jax.numpy as jnp
from jax import lax

D = 4096
HEADS = 16
HEAD = 128
HD = 2048
LENGTH = 1024
BATCH = 16


def base_draw(key, salt):
    inner = jax.random.fold_in(key, salt)
    return jax.random.truncated_normal(inner, -6.0, 6.0, (BATCH, LENGTH, HD), jnp.float32)


def draw_query_input(key, part):
    values = base_draw(key, 21)
    return values.astype(jnp.bfloat16)


def draw_key_input(key, part):
    values = base_draw(key, 22)
    return values.astype(jnp.bfloat16)


def spiked(values, own_key, source, target, parts, factor):
    owner, partner = [(jnp.arange(values.shape[axis_at]) // (values.shape[axis_at] // parts)).reshape([-1 if axis == axis_at else 1 for axis in range(values.ndim)]) for axis_at in (source, target)]
    chosen = jax.random.permutation(own_key, parts)[partner]
    strong = (owner == chosen) | (owner == (partner + parts // 2) % parts)
    return jnp.where(strong, factor * values, values)


def levels(own_key, shape, split, low, high):
    factor_of, own = 1.0, jax.random.fold_in(own_key, 6)
    for dim, shards_of in split:
        draws = jnp.exp(jax.random.uniform(jax.random.fold_in(own, dim), (shards_of,), jnp.float32, low / len(split), high / len(split)))
        factor_of = factor_of * jnp.repeat(draws, shape[dim] // shards_of).reshape([-1 if axis == dim else 1 for axis in range(len(shape))])
    return factor_of


def gaussian(rng, shape, deviation, bound, pieces=(), dtype=jnp.bfloat16):
    result = deviation * jax.random.normal(rng, shape, jnp.float32)
    if pieces:
        result = result * levels(rng, shape, pieces, -0.22, 0.18)
    return jnp.clip(result, -bound, bound).astype(dtype)


def gaussian_with(own_key, dims, spread, bound, shards, heavy, held_as=jnp.bfloat16):
    entries = spread * jax.random.normal(own_key, dims, jnp.float32)
    if shards:
        entries = entries * levels(own_key, dims, shards, -0.22, 0.18)
    return jnp.clip(spiked(entries, jax.random.fold_in(own_key, 3), *heavy), -bound, bound).astype(held_as)


def setup_inputs(seed: int = 0) -> dict:
    arg_keys = jax.random.split(jax.random.key(seed), 6)
    return {
        "query_input": draw_query_input(jax.random.fold_in(arg_keys[5], 71), 0),
        "key_input": draw_key_input(jax.random.fold_in(arg_keys[5], 71), 0),
        "value_input": gaussian(arg_keys[2], (BATCH, LENGTH, HD), 1.0, 6.0, ((0, 16), (1, 8))),
        "out_weight": gaussian(arg_keys[3], (HD, D), HD ** -0.5, 0.125, ((1, 16),)),
        "grad_out": gaussian_with(arg_keys[4], (BATCH, LENGTH, D), 1.0, 6.0, ((0, 16), (1, 8)), (0, 2, 16, 2.0)),
    }


def probs_of(query_rows, key_rows, score_scale):
    scores = jnp.dot(query_rows, key_rows.T, preferred_element_type=jnp.float32) * score_scale
    row_peak = jnp.max(scores, axis=1, keepdims=True)
    shifted = jnp.exp(scores - row_peak)
    return shifted / jnp.sum(shifted, axis=1, keepdims=True)


def reference(query_input, key_input, value_input, out_weight, grad_out):
    score_scale = HEAD ** -0.5

    def heads_of(matrix):
        return matrix.reshape(LENGTH, HEADS, HEAD).transpose(1, 0, 2)

    def join_heads(matrix):
        return matrix.transpose(1, 0, 2).reshape(LENGTH, HD)

    def one_batch(weight_accum, batch_items):
        query_rows, key_rows, value_rows, grad_rows = batch_items
        query_heads = heads_of(query_rows)
        key_heads = heads_of(key_rows)
        value_heads = heads_of(value_rows)

        def forward_head(triple):
            query_one, key_one, value_one = triple
            prob_rows = probs_of(query_one, key_one, score_scale)
            return jnp.dot(prob_rows.astype(jnp.bfloat16), value_one, preferred_element_type=jnp.float32).astype(jnp.bfloat16)

        attended = join_heads(lax.map(forward_head, (query_heads, key_heads, value_heads)))
        projected = jnp.dot(attended, out_weight, preferred_element_type=jnp.float32).astype(jnp.bfloat16)
        grad_attended = jnp.dot(grad_rows, out_weight.T, preferred_element_type=jnp.float32).astype(jnp.bfloat16)
        weight_accum = weight_accum + jnp.dot(attended.T, grad_rows, preferred_element_type=jnp.float32)
        grad_heads = heads_of(grad_attended)

        def backward_head(quadruple):
            query_one, key_one, value_one, grad_one = quadruple
            prob_rows = probs_of(query_one, key_one, score_scale)
            prob_low = prob_rows.astype(jnp.bfloat16)
            grad_value = jnp.dot(prob_low.T, grad_one, preferred_element_type=jnp.float32).astype(jnp.bfloat16)
            grad_prob = jnp.dot(grad_one, value_one.T, preferred_element_type=jnp.float32)
            row_delta = jnp.sum(prob_rows * grad_prob, axis=1, keepdims=True)
            grad_score = (prob_rows * (grad_prob - row_delta) * score_scale).astype(jnp.bfloat16)
            grad_query = jnp.dot(grad_score, key_one, preferred_element_type=jnp.float32).astype(jnp.bfloat16)
            grad_key = jnp.dot(grad_score.T, query_one, preferred_element_type=jnp.float32).astype(jnp.bfloat16)
            return grad_query, grad_key, grad_value

        grad_query, grad_key, grad_value = lax.map(backward_head, (query_heads, key_heads, value_heads, grad_heads))
        return weight_accum, (projected, join_heads(grad_query), join_heads(grad_key), join_heads(grad_value))

    zero_grad = jnp.zeros((HD, D), jnp.float32)
    grad_weight, outputs = lax.scan(one_batch, zero_grad, (query_input, key_input, value_input, grad_out))
    projected, grad_query, grad_key, grad_value = outputs
    return projected, grad_query, grad_key, grad_value, grad_weight
```

```python
import jax
import jax.numpy as jnp
from jax import lax
from jax.experimental import pallas as pl
from jax.experimental.pallas import tpu as pltpu
from jax.sharding import PartitionSpec as P

HEAD = 128
X = 4
BLOCK = 256
SCALE = HEAD ** (-0.5)
MIB = 1 << 20


def params(mib):
    return pltpu.CompilerParams(vmem_limit_bytes=mib * MIB)


def cost(flops, size, trans=0):
    return pl.CostEstimate(flops=flops, bytes_accessed=size, transcendentals=trans)


def nt(a, b):
    return lax.dot_general(a, b, (((1,), (1,)), ((), ())), preferred_element_type=jnp.float32)


def tn(a, b):
    return lax.dot_general(a, b, (((0,), (0,)), ((), ())), preferred_element_type=jnp.float32)


def run_copies(pairs, sems):
    copies = [pltpu.make_async_copy(a, b, sems.at[i]) for i, (a, b) in enumerate(pairs)]
    for copy in copies:
        copy.start()
    for copy in copies:
        copy.wait()


ANY = pl.BlockSpec(memory_space=pl.ANY)


def place():
    me = lax.axis_index("dp")
    return me // (2 * X), (me // 2) % X, me % 2


def column_of(yl, x, core, j):
    other_y, other_core = j // 2, j % 2
    yy = yl + other_y - 2 * yl * other_y
    cc = core + other_core - 2 * core * other_core
    return pl.multiple_of(((yy * X + x) * 2 + cc) * BLOCK, BLOCK)


def pack_qkv(query, key, value):
    tok, feat = query.shape
    groups = feat // BLOCK

    def body(q, k, v, out, sems):
        run_copies(
            [
                (src.at[:, pl.ds(g * BLOCK, BLOCK)], out.at[g, i])
                for g in range(groups)
                for i, src in enumerate((q, k, v))
            ],
            sems,
        )

    return pl.pallas_call(
        body,
        out_shape=jax.ShapeDtypeStruct((groups, 3, tok, BLOCK), query.dtype),
        in_specs=[ANY] * 3,
        out_specs=ANY,
        scratch_shapes=[pltpu.SemaphoreType.DMA((groups * 3,))],
        cost_estimate=cost(0, 3 * 2 * 2 * tok * feat),
        name="pack_qkv",
    )(query, key, value)


def pack_grad(grad):
    tok, cols = grad.shape

    def body(src, *rest):
        outs, sems = rest[:X], rest[X]
        yl, x, core = place()
        run_copies(
            [
                (
                    src.at[:, pl.ds(column_of(yl, (x + s) % X, core, j), BLOCK)],
                    outs[s].at[:, pl.ds(j * BLOCK, BLOCK)],
                )
                for s in range(X)
                for j in range(4)
            ],
            sems,
        )

    return pl.pallas_call(
        body,
        out_shape=[jax.ShapeDtypeStruct((tok, 4 * BLOCK), grad.dtype)] * X,
        in_specs=[ANY],
        out_specs=[ANY] * X,
        scratch_shapes=[pltpu.SemaphoreType.DMA((16,))],
        cost_estimate=cost(0, 4 * tok * cols),
        name="pack_grad",
    )(grad)


def place_projected(parts, cols):
    tok = parts[0].shape[0]

    def body(*refs):
        srcs, out, sems = refs[:X], refs[X], refs[X + 1]
        yl, x, core = place()
        run_copies(
            [
                (
                    srcs[s].at[:, pl.ds(j * BLOCK, BLOCK)],
                    out.at[:, pl.ds(column_of(yl, (x + s) % X, core, j), BLOCK)],
                )
                for s in range(X)
                for j in range(4)
            ],
            sems,
        )

    return pl.pallas_call(
        body,
        out_shape=jax.ShapeDtypeStruct((tok, cols), parts[0].dtype),
        in_specs=[ANY] * X,
        out_specs=ANY,
        scratch_shapes=[pltpu.SemaphoreType.DMA((16,))],
        cost_estimate=cost(0, 4 * tok * cols),
        name="place_projected",
    )(*parts)


def head_spec(groups, tok, i):
    return pl.BlockSpec((groups, pl.squeezed, tok, HEAD), lambda h: (0, i, 0, h))


def attend(qkv):
    groups, _, tok, width = qkv.shape
    heads, length = width // HEAD, groups * tok
    rows = 256

    def body(q_ref, k_ref, v_ref, o_ref, lse_ref):
        keys = k_ref[...].reshape(length, HEAD)
        values = v_ref[...].reshape(length, HEAD)
        for b in range(length // rows):
            per = rows // tok
            query = q_ref[b * per : (b + 1) * per].reshape(rows, HEAD)
            scores = nt(keys, query) * SCALE
            peak = jnp.max(scores, axis=0, keepdims=True)
            shifted = jnp.exp(scores - peak)
            total = jnp.sum(shifted, axis=0, keepdims=True)
            out = tn(values, shifted.astype(jnp.bfloat16)) / total
            o_ref[b * per : (b + 1) * per] = out.T.astype(jnp.bfloat16).reshape(per, tok, HEAD)
            lse_ref[:, b * rows : (b + 1) * rows] = peak + jnp.log(total)

    return pl.pallas_call(
        body,
        grid=(heads,),
        out_shape=[
            jax.ShapeDtypeStruct((groups, tok, width), jnp.bfloat16),
            jax.ShapeDtypeStruct((heads, 1, length), jnp.float32),
        ],
        in_specs=[head_spec(groups, tok, i) for i in range(3)],
        out_specs=[
            pl.BlockSpec((groups, tok, HEAD), lambda h: (0, 0, h)),
            pl.BlockSpec((pl.squeezed, 1, length), lambda h: (h, 0, 0)),
        ],
        compiler_params=params(32),
        cost_estimate=cost(8 * heads * length * length * HEAD, 8 * length * width, heads * length * length),
        name="attend",
    )(qkv, qkv, qkv)


def attend_back(qkv, lse, grad):
    groups, _, tok, width = qkv.shape
    heads, length = width // HEAD, groups * tok
    rows = 256

    def body(q_ref, k_ref, v_ref, lse_ref, g_ref, dq_ref, dk_ref, dv_ref, k_acc, v_acc):
        keys = k_ref[...].reshape(length, HEAD)
        values = v_ref[...].reshape(length, HEAD)
        for b in range(length // rows):
            per = rows // tok
            query = q_ref[b * per : (b + 1) * per].reshape(rows, HEAD)
            grad_rows = g_ref[b * per : (b + 1) * per].reshape(rows, HEAD)
            scores = nt(keys, query) * SCALE
            probs = jnp.exp(scores - lse_ref[:, b * rows : (b + 1) * rows])
            grad_probs = nt(values, grad_rows)
            delta = jnp.sum(probs * grad_probs, axis=0, keepdims=True)
            grad_scores = (probs * (grad_probs - delta)).astype(jnp.bfloat16)
            dv = jnp.dot(probs.astype(jnp.bfloat16), grad_rows, preferred_element_type=jnp.float32)
            dk = jnp.dot(grad_scores, query, preferred_element_type=jnp.float32)
            if b == 0:
                v_acc[...] = dv
                k_acc[...] = dk
            else:
                v_acc[...] += dv
                k_acc[...] += dk
            dq = tn(keys, grad_scores) * SCALE
            dq_ref[b * rows : (b + 1) * rows, :] = dq.T.astype(jnp.bfloat16)
        dk_ref[...] = (k_acc[...] * SCALE).astype(jnp.bfloat16)
        dv_ref[...] = v_acc[...].astype(jnp.bfloat16)

    out = jax.ShapeDtypeStruct((length, width), jnp.bfloat16)
    return pl.pallas_call(
        body,
        grid=(heads,),
        out_shape=[out] * 3,
        in_specs=[head_spec(groups, tok, i) for i in range(3)]
        + [
            pl.BlockSpec((pl.squeezed, 1, length), lambda h: (h, 0, 0)),
            pl.BlockSpec((groups, tok, HEAD), lambda h: (0, 0, h)),
        ],
        out_specs=[pl.BlockSpec((length, HEAD), lambda h: (0, h))] * 3,
        scratch_shapes=[pltpu.VMEM((length, HEAD), jnp.float32)] * 2,
        compiler_params=params(40),
        cost_estimate=cost(20 * heads * length * length * HEAD, 14 * length * width, heads * length * length),
        name="attend_back",
    )(qkv, qkv, qkv, lse, grad)


def grad_attended_parts(grads, weights):
    tok, width = grads[0].shape
    feat, block = weights[0].shape
    groups = feat // BLOCK

    def body(*refs):
        g_refs, w_refs, outs = refs[:X], refs[X : X + 4], refs[X + 4 :]
        total = None
        for j in range(4):
            cols = jnp.concatenate([g[:, j * block : (j + 1) * block] for g in g_refs], axis=0)
            term = nt(cols, w_refs[j][...])
            total = term if total is None else total + term
        total = total.astype(jnp.bfloat16)
        for s in range(X):
            outs[s][...] = total[s * tok : (s + 1) * tok]

    return pl.pallas_call(
        body,
        grid=(groups,),
        out_shape=[jax.ShapeDtypeStruct((groups, tok, BLOCK), jnp.bfloat16)] * X,
        in_specs=[pl.BlockSpec((tok, width), lambda n: (0, 0))] * X
        + [pl.BlockSpec((BLOCK, block), lambda n: (n, 0))] * 4,
        out_specs=[pl.BlockSpec((pl.squeezed, tok, BLOCK), lambda n: (n, 0, 0))] * X,
        compiler_params=params(32),
        cost_estimate=cost(2 * X * tok * width * feat, 2 * feat * width + 4 * X * tok * width),
        name="grad_attended",
    )(*grads, *weights)


def project(attended, grads, weights):
    groups, tok, block = attended[0].shape
    width = grads[0].shape[1]

    def body(*refs):
        a_refs, g_refs, w_refs = refs[:X], refs[X : 2 * X], refs[2 * X : 2 * X + 4]
        outs, near, far, acc = refs[2 * X + 4 : 3 * X + 4], *refs[3 * X + 4 :]
        n = pl.program_id(0)
        rows = jnp.concatenate([a[...] for a in a_refs], axis=0)
        for j in range(4):
            cols = slice(j * block, (j + 1) * block)
            term = jnp.dot(rows, w_refs[j][...], preferred_element_type=jnp.float32)

            @pl.when(n == 0)
            def _():
                acc[:, cols] = term

            @pl.when(n > 0)
            def _():
                acc[:, cols] += term

            grad_cols = jnp.concatenate([g[:, cols] for g in g_refs], axis=0)
            piece = tn(rows, grad_cols).astype(jnp.bfloat16)
            (near, far)[j % 2][j // 2] = piece

        @pl.when(n == groups - 1)
        def _():
            for s in range(X):
                outs[s][...] = acc[s * tok : (s + 1) * tok].astype(jnp.bfloat16)

    return pl.pallas_call(
        body,
        grid=(groups,),
        out_shape=[jax.ShapeDtypeStruct((tok, width), jnp.bfloat16)] * X
        + [jax.ShapeDtypeStruct((groups, 2, block, block), jnp.bfloat16)] * 2,
        in_specs=[pl.BlockSpec((pl.squeezed, tok, block), lambda n: (n, 0, 0))] * X
        + [pl.BlockSpec((tok, width), lambda n: (0, 0))] * X
        + [pl.BlockSpec((block, block), lambda n: (n, 0))] * 4,
        out_specs=[pl.BlockSpec((tok, width), lambda n: (0, 0))] * X
        + [pl.BlockSpec((pl.squeezed, 2, block, block), lambda n: (n, 0, 0, 0))] * 2,
        scratch_shapes=[pltpu.VMEM((X * tok, width), jnp.float32)],
        compiler_params=params(32),
        cost_estimate=cost(4 * X * tok * width * groups * block, 12 * MIB),
        name="project",
    )(*attended, *grads, *weights)


def shift_x(array, shift, count):
    pairs = []
    for d in range(count):
        x = (d // 2) % X
        pairs.append((d, d + 2 * ((x + shift) % X - x)))
    return lax.ppermute(array, "dp", pairs)


def swap(array, bit, count):
    return lax.ppermute(array, "dp", [(d, d ^ bit) for d in range(count)])


def exchange(array):
    return lax.all_to_all(array, "seq", 0, 0, tiled=False)


def f32_sum(*arrays):
    total = arrays[0].astype(jnp.float32)
    for array in arrays[1:]:
        total = total + array.astype(jnp.float32)
    return total


def shards(query_input, key_input, value_input, out_weight, grad_out):
    dp = lax.axis_size("dp")
    cols = grad_out.shape[2]
    qkv = exchange(pack_qkv(query_input[0], key_input[0], value_input[0]))

    mine = pack_grad(grad_out[0])
    grads = [mine[0]] + [shift_x(mine[s], s, dp) for s in range(1, X)]
    far_weight = swap(out_weight, 2 * X, dp)
    weights = [out_weight, swap(out_weight, 1, dp), far_weight, swap(far_weight, 1, dp)]

    parts = grad_attended_parts(grads, weights)
    parts = [parts[0]] + [shift_x(parts[s], -s, dp) for s in range(1, X)]
    grad_attended = exchange(f32_sum(*parts).astype(jnp.bfloat16))

    attended, lse = attend(qkv)
    attended = exchange(attended)
    rows = [attended] + [shift_x(attended, s, dp) for s in range(1, X)]
    *projected, near, far = project(rows, grads, weights)
    projected = [projected[0]] + [shift_x(projected[s], -s, dp) for s in range(1, X)]
    projected = place_projected(projected, cols)[None]

    weight_sum = f32_sum(near, swap(far, 1, dp)).astype(jnp.bfloat16)
    weight_sum = jnp.sum(exchange(weight_sum).astype(jnp.float32), axis=0)
    grad_weight = weight_sum[0] + swap(weight_sum[1].astype(jnp.bfloat16), 2 * X, dp).astype(
        jnp.float32
    )

    grads_in = attend_back(qkv, lse, grad_attended)
    return (projected, *[g[None] for g in grads_in], grad_weight)


def solution(mesh):
    return jax.shard_map(
        shards,
        mesh=mesh,
        in_specs=(
            P("dp", "seq", None),
            P("dp", "seq", None),
            P("dp", "seq", None),
            P(None, "dp"),
            P("dp", "seq", None),
        ),
        out_specs=(
            P("dp", "seq", None),
            P("dp", None, "seq"),
            P("dp", None, "seq"),
            P("dp", None, "seq"),
            P("seq", "dp"),
        ),
        check_vma=False,
    )
```

```python
import jax
import jax.numpy as jnp
from jax import lax
from jax.experimental import pallas as pl
from jax.experimental.pallas import tpu as pltpu
from jax.sharding import Mesh
from jax.sharding import PartitionSpec as P

HEAD = 128
X = 4
DP = ("yl", "x", "core")
SEQ = ("z", "yh")
BLOCK = 256
SCALE = HEAD ** (-0.5)
MIB = 1 << 20


def params(mib):
    return pltpu.CompilerParams(vmem_limit_bytes=mib * MIB)


def cost(flops, size, trans=0):
    return pl.CostEstimate(flops=flops, bytes_accessed=size, transcendentals=trans)


def nt(a, b):
    return lax.dot_general(a, b, (((1,), (1,)), ((), ())), preferred_element_type=jnp.float32)


def tn(a, b):
    return lax.dot_general(a, b, (((0,), (0,)), ((), ())), preferred_element_type=jnp.float32)


def place():
    return tuple(lax.axis_index(name) for name in DP)


def column_of(yl, x, core, j):
    other_y, other_core = j // 2, j % 2
    yy = yl + other_y - 2 * yl * other_y
    cc = core + other_core - 2 * core * other_core
    return pl.multiple_of(((yy * X + x) * 2 + cc) * BLOCK, BLOCK)


def pack_qkv(query, key, value):
    tok, feat = query.shape
    groups = feat // BLOCK

    def body(q, k, v, out):
        for g in range(groups):
            for i, src in enumerate((q, k, v)):
                out[g, i] = src[:, g * BLOCK : (g + 1) * BLOCK]

    return pl.pallas_call(
        body,
        out_shape=jax.ShapeDtypeStruct((groups, 3, tok, BLOCK), query.dtype),
        compiler_params=params(16),
        cost_estimate=cost(0, 3 * 2 * 2 * tok * feat),
        name="pack_qkv",
    )(query, key, value)


def pack_grad(grad):
    tok, cols = grad.shape

    def body(src, *outs):
        yl, x, core = place()
        for s in range(X):
            for j in range(4):
                outs[s][:, j * BLOCK : (j + 1) * BLOCK] = src[
                    :, pl.ds(column_of(yl, (x + s) % X, core, j), BLOCK)
                ]

    return pl.pallas_call(
        body,
        out_shape=[jax.ShapeDtypeStruct((tok, 4 * BLOCK), grad.dtype)] * X,
        compiler_params=params(16),
        cost_estimate=cost(0, 4 * tok * cols),
        name="pack_grad",
    )(grad)


def place_projected(parts, cols):
    tok = parts[0].shape[0]

    def body(*refs):
        srcs, out = refs[:X], refs[X]
        yl, x, core = place()
        for s in range(X):
            for j in range(4):
                out[:, pl.ds(column_of(yl, (x + s) % X, core, j), BLOCK)] = srcs[s][
                    :, j * BLOCK : (j + 1) * BLOCK
                ]

    return pl.pallas_call(
        body,
        out_shape=jax.ShapeDtypeStruct((tok, cols), parts[0].dtype),
        compiler_params=params(16),
        cost_estimate=cost(0, 4 * tok * cols),
        name="place_projected",
    )(*parts)


def head_spec(groups, tok, i):
    return pl.BlockSpec((groups, pl.squeezed, tok, HEAD), lambda h: (0, i, 0, h))


def attend(qkv):
    groups, _, tok, width = qkv.shape
    heads, length = width // HEAD, groups * tok
    rows = 256

    def body(q_ref, k_ref, v_ref, o_ref, lse_ref):
        keys = k_ref[...].reshape(length, HEAD)
        values = v_ref[...].reshape(length, HEAD)
        for b in range(length // rows):
            per = rows // tok
            query = q_ref[b * per : (b + 1) * per].reshape(rows, HEAD)
            scores = nt(keys, query) * SCALE
            peak = jnp.max(scores, axis=0, keepdims=True)
            shifted = jnp.exp(scores - peak)
            total = jnp.sum(shifted, axis=0, keepdims=True)
            out = tn(values, shifted.astype(jnp.bfloat16)) / total
            o_ref[b * per : (b + 1) * per] = out.T.astype(jnp.bfloat16).reshape(per, tok, HEAD)
            lse_ref[:, b * rows : (b + 1) * rows] = peak + jnp.log(total)

    return pl.pallas_call(
        body,
        grid=(heads,),
        out_shape=[
            jax.ShapeDtypeStruct((groups, tok, width), jnp.bfloat16),
            jax.ShapeDtypeStruct((heads, 1, length), jnp.float32),
        ],
        in_specs=[head_spec(groups, tok, i) for i in range(3)],
        out_specs=[
            pl.BlockSpec((groups, tok, HEAD), lambda h: (0, 0, h)),
            pl.BlockSpec((pl.squeezed, 1, length), lambda h: (h, 0, 0)),
        ],
        compiler_params=params(32),
        cost_estimate=cost(8 * heads * length * length * HEAD, 8 * length * width, heads * length * length),
        name="attend",
    )(qkv, qkv, qkv)


def attend_back(qkv, lse, grad):
    groups, _, tok, width = qkv.shape
    heads, length = width // HEAD, groups * tok
    rows = 256

    def body(q_ref, k_ref, v_ref, lse_ref, g_ref, dq_ref, dk_ref, dv_ref, k_acc, v_acc):
        keys = k_ref[...].reshape(length, HEAD)
        values = v_ref[...].reshape(length, HEAD)
        for b in range(length // rows):
            per = rows // tok
            query = q_ref[b * per : (b + 1) * per].reshape(rows, HEAD)
            grad_rows = g_ref[b * per : (b + 1) * per].reshape(rows, HEAD)
            scores = nt(keys, query) * SCALE
            probs = jnp.exp(scores - lse_ref[:, b * rows : (b + 1) * rows])
            grad_probs = nt(values, grad_rows)
            delta = jnp.sum(probs * grad_probs, axis=0, keepdims=True)
            grad_scores = (probs * (grad_probs - delta)).astype(jnp.bfloat16)
            dv = jnp.dot(probs.astype(jnp.bfloat16), grad_rows, preferred_element_type=jnp.float32)
            dk = jnp.dot(grad_scores, query, preferred_element_type=jnp.float32)
            if b == 0:
                v_acc[...] = dv
                k_acc[...] = dk
            else:
                v_acc[...] += dv
                k_acc[...] += dk
            dq = tn(keys, grad_scores) * SCALE
            dq_ref[b * rows : (b + 1) * rows, :] = dq.T.astype(jnp.bfloat16)
        dk_ref[...] = (k_acc[...] * SCALE).astype(jnp.bfloat16)
        dv_ref[...] = v_acc[...].astype(jnp.bfloat16)

    out = jax.ShapeDtypeStruct((length, width), jnp.bfloat16)
    return pl.pallas_call(
        body,
        grid=(heads,),
        out_shape=[out] * 3,
        in_specs=[head_spec(groups, tok, i) for i in range(3)]
        + [
            pl.BlockSpec((pl.squeezed, 1, length), lambda h: (h, 0, 0)),
            pl.BlockSpec((groups, tok, HEAD), lambda h: (0, 0, h)),
        ],
        out_specs=[pl.BlockSpec((length, HEAD), lambda h: (0, h))] * 3,
        scratch_shapes=[pltpu.VMEM((length, HEAD), jnp.float32)] * 2,
        compiler_params=params(40),
        cost_estimate=cost(20 * heads * length * length * HEAD, 14 * length * width, heads * length * length),
        name="attend_back",
    )(qkv, qkv, qkv, lse, grad)


def grad_attended_parts(grads, weights):
    rows, width = grads.shape
    tok = rows // X
    _, feat, block = weights.shape
    groups = feat // BLOCK

    def body(g_ref, w_ref, *outs):
        total = None
        for j in range(4):
            term = nt(g_ref[:, j * block : (j + 1) * block], w_ref[j])
            total = term if total is None else total + term
        total = total.astype(jnp.bfloat16)
        for s in range(X):
            outs[s][...] = total[s * tok : (s + 1) * tok]

    return pl.pallas_call(
        body,
        grid=(groups,),
        out_shape=[jax.ShapeDtypeStruct((groups, tok, BLOCK), jnp.bfloat16)] * X,
        in_specs=[
            pl.BlockSpec((rows, width), lambda n: (0, 0)),
            pl.BlockSpec((4, BLOCK, block), lambda n: (0, n, 0)),
        ],
        out_specs=[pl.BlockSpec((pl.squeezed, tok, BLOCK), lambda n: (n, 0, 0))] * X,
        compiler_params=params(32),
        cost_estimate=cost(2 * rows * width * feat, 2 * feat * width + 4 * rows * width),
        name="grad_attended",
    )(grads, weights)


def weight_parts(attended, grads, core):
    groups, tok, block = attended[0].shape
    rows = X * tok

    def body(*refs):
        a_refs, g_ref, out, cols = refs[:X], refs[X], refs[X + 1], refs[X + 2]

        @pl.when(pl.program_id(0) == 0)
        def _():
            for i in range(2):
                j = 2 * i + core
                cols[:, i * block : (i + 1) * block] = g_ref[:, j * block : (j + 1) * block]

        left = jnp.concatenate([a[...] for a in a_refs], axis=0)
        piece = tn(left, cols[...]).astype(jnp.bfloat16)
        yl = lax.axis_index("yl")
        for i in range(2):
            out[yl + i - 2 * yl * i] = piece[:, i * block : (i + 1) * block]

    return pl.pallas_call(
        body,
        grid=(groups,),
        out_shape=jax.ShapeDtypeStruct((2, groups, block, block), jnp.bfloat16),
        in_specs=[pl.BlockSpec((pl.squeezed, tok, block), lambda n: (n, 0, 0))] * X
        + [pl.BlockSpec(grads.shape, lambda n: (0, 0))],
        out_specs=pl.BlockSpec((2, pl.squeezed, block, block), lambda n: (0, n, 0, 0)),
        scratch_shapes=[pltpu.VMEM((rows, 2 * block), jnp.bfloat16)],
        compiler_params=params(24),
        cost_estimate=cost(4 * rows * groups * block * block, 5 * MIB),
        name="weight_parts",
    )(*attended, grads)


def project(attended, weights):
    groups, tok, block = attended[0].shape
    rows, feat = X * tok, groups * block

    def body(*refs):
        a_refs, w_ref, outs, left = refs[:X], refs[X], refs[X + 1 : 2 * X + 1], refs[2 * X + 1]

        @pl.when(pl.program_id(0) == 0)
        def _():
            for s in range(X):
                for n in range(groups):
                    left[s * tok : (s + 1) * tok, n * block : (n + 1) * block] = a_refs[s][n]

        out = jnp.dot(left[...], w_ref[...], preferred_element_type=jnp.float32)
        out = out.astype(jnp.bfloat16)
        for s in range(X):
            outs[s][...] = out[s * tok : (s + 1) * tok]

    return pl.pallas_call(
        body,
        grid=(4,),
        out_shape=[jax.ShapeDtypeStruct((tok, 4 * block), jnp.bfloat16)] * X,
        in_specs=[pl.BlockSpec((groups, tok, block), lambda j: (0, 0, 0))] * X
        + [pl.BlockSpec((pl.squeezed, feat, block), lambda j: (j, 0, 0))],
        out_specs=[pl.BlockSpec((tok, block), lambda j: (0, j))] * X,
        scratch_shapes=[pltpu.VMEM((rows, feat), jnp.bfloat16)],
        compiler_params=params(24),
        cost_estimate=cost(8 * rows * feat * block, 7 * MIB),
        name="project",
    )(*attended, weights)


def shift_x(array, shift):
    return lax.ppermute(array, "x", [(i, (i + shift) % X) for i in range(X)])


def swap(array, axis):
    return lax.ppermute(array, axis, [(0, 1), (1, 0)])


def exchange(array, axes=SEQ):
    return lax.all_to_all(array, axes, 0, 0, tiled=False)


def after(arrays, *others):
    return lax.optimization_barrier((arrays, others))[0]


def f32_sum(*arrays):
    total = arrays[0].astype(jnp.float32)
    for array in arrays[1:]:
        total = total + array.astype(jnp.float32)
    return total


def shards(query_input, key_input, value_input, out_weight, grad_out):
    cols = grad_out.shape[2]
    half = out_weight.shape[0] // 2

    lower, upper = lax.optimization_barrier((out_weight[:half], out_weight[half:]))
    query, key, value = after((query_input[0], key_input[0], value_input[0]), lower, upper)
    lower = swap(lower, "yl")
    upper = lax.ppermute(upper, ("yl", "yh"), [(i, 3 - i) for i in range(4)])
    qkv = exchange(pack_qkv(query, key, value))
    mine = pack_grad(grad_out[0])
    grads = [mine[0]] + [shift_x(mine[s], s) for s in range(1, X)]
    grads = jnp.concatenate(grads, axis=0)
    weights = [out_weight, swap(out_weight, "core")]
    weights.append(jnp.concatenate([lower, upper], axis=0))
    weights.append(jnp.concatenate([swap(lower, "core"), swap(upper, "core")], axis=0))
    weights = jnp.stack(weights)
    parts = grad_attended_parts(grads, weights)

    attended, lse = attend(after(qkv, *parts))
    parts = [parts[0]] + [shift_x(parts[s], -s) for s in range(1, X)]
    attended = after(exchange(attended), *parts)
    rows = [attended] + [shift_x(attended, s) for s in range(1, X)]
    grad_attended = exchange(f32_sum(*parts).astype(jnp.bfloat16))

    grads = after(grads, grad_attended)
    far = swap(weight_parts(rows, grads, 1), "core")
    near = weight_parts(rows, grads, 0)
    total = f32_sum(near, far).astype(jnp.bfloat16)
    total = exchange(total.reshape(-1, BLOCK, BLOCK), ("yl", *SEQ))
    grad_weight = jnp.sum(total.astype(jnp.float32), axis=0)

    projected = project(rows, weights)
    projected = [projected[0]] + [shift_x(projected[s], -s) for s in range(1, X)]
    projected = place_projected(projected, cols)[None]

    grads_in = attend_back(qkv, lse, grad_attended)
    return (projected, *[g[None] for g in grads_in], grad_weight)


def solution(mesh):
    fine = Mesh(mesh.devices.reshape(-1, X, 2, X, 2), DP + SEQ)
    return jax.shard_map(
        shards,
        mesh=fine,
        in_specs=(P(DP, SEQ, None), P(DP, SEQ, None), P(DP, SEQ, None), P(None, DP), P(DP, SEQ, None)),
        out_specs=(P(DP, SEQ, None), P(DP, None, SEQ), P(DP, None, SEQ), P(DP, None, SEQ), P(SEQ, DP)),
        check_vma=False,
    )
```

```python
import jax
import jax.numpy as jnp
from jax import lax
from jax.experimental import pallas as pl
from jax.experimental.pallas import tpu as pltpu
from jax.sharding import Mesh
from jax.sharding import PartitionSpec as P

HEAD = 128
X = 4
DP = ("yl", "x", "core")
SEQ = ("z", "yh")
BLOCK = 256
SCALE = HEAD ** (-0.5)
LOG2E = 1.4426950408889634
MIB = 1 << 20


def params(mib):
    return pltpu.CompilerParams(vmem_limit_bytes=mib * MIB)


def cost(flops, size, trans=0):
    return pl.CostEstimate(flops=flops, bytes_accessed=size, transcendentals=trans)


def nt(a, b):
    return lax.dot_general(a, b, (((1,), (1,)), ((), ())), preferred_element_type=jnp.float32)


def tn(a, b):
    return lax.dot_general(a, b, (((0,), (0,)), ((), ())), preferred_element_type=jnp.float32)


def place():
    return tuple(lax.axis_index(name) for name in DP)


def column_of(yl, x, core, j):
    other_y, other_core = j // 2, j % 2
    yy = yl + other_y - 2 * yl * other_y
    cc = core + other_core - 2 * core * other_core
    return pl.multiple_of(((yy * X + x) * 2 + cc) * BLOCK, BLOCK)


def pack_qkv(query, key, value):
    tok, feat = query.shape
    groups = feat // BLOCK

    def body(q, k, v, out):
        for g in range(groups):
            for i, src in enumerate((q, k, v)):
                out[g, i] = src[:, g * BLOCK : (g + 1) * BLOCK]

    return pl.pallas_call(
        body,
        out_shape=jax.ShapeDtypeStruct((groups, 3, tok, BLOCK), query.dtype),
        compiler_params=params(16),
        cost_estimate=cost(0, 3 * 2 * 2 * tok * feat),
        name="pack_qkv",
    )(query, key, value)


def pack_grad(grad):
    tok, cols = grad.shape

    def body(src, *outs):
        yl, x, core = place()
        for s in range(X):
            for j in range(4):
                outs[s][:, j * BLOCK : (j + 1) * BLOCK] = src[
                    :, pl.ds(column_of(yl, (x + s) % X, core, j), BLOCK)
                ]

    return pl.pallas_call(
        body,
        out_shape=[jax.ShapeDtypeStruct((tok, 4 * BLOCK), grad.dtype)] * X,
        compiler_params=params(16),
        cost_estimate=cost(0, 4 * tok * cols),
        name="pack_grad",
    )(grad)


def place_projected(parts, cols):
    tok = parts[0].shape[0]

    def body(*refs):
        srcs, out = refs[:X], refs[X]
        yl, x, core = place()
        for s in range(X):
            for j in range(4):
                out[:, pl.ds(column_of(yl, (x + s) % X, core, j), BLOCK)] = srcs[s][
                    :, j * BLOCK : (j + 1) * BLOCK
                ]

    return pl.pallas_call(
        body,
        out_shape=jax.ShapeDtypeStruct((tok, cols), parts[0].dtype),
        compiler_params=params(16),
        cost_estimate=cost(0, 4 * tok * cols),
        name="place_projected",
    )(*parts)


def head_spec(groups, tok, i):
    return pl.BlockSpec((groups, pl.squeezed, tok, HEAD), lambda h: (0, i, 0, h))


def attend(qkv):
    groups, _, tok, width = qkv.shape
    heads, length = width // HEAD, groups * tok

    def body(q_ref, k_ref, v_ref, o_ref, lse_ref):
        for h in range(heads):
            cols = slice(h * HEAD, (h + 1) * HEAD)
            keys = k_ref[:, :, cols].reshape(length, HEAD)
            values = v_ref[:, :, cols].reshape(length, HEAD)
            for b in range(groups):
                scores = nt(keys, q_ref[b, :, cols]) * (SCALE * LOG2E)
                peak = jnp.max(scores, axis=0, keepdims=True)
                shifted = jnp.exp2(scores - peak)
                total = jnp.sum(shifted, axis=0, keepdims=True)
                out = tn(values, shifted.astype(jnp.bfloat16)) / total
                o_ref[b, :, cols] = out.T.astype(jnp.bfloat16)
                lse_ref[h, :, b * tok : (b + 1) * tok] = peak + jnp.log2(total)

    return pl.pallas_call(
        body,
        grid=(1,),
        out_shape=[
            jax.ShapeDtypeStruct((groups, tok, width), jnp.bfloat16),
            jax.ShapeDtypeStruct((heads, 1, length), jnp.float32),
        ],
        in_specs=[
            pl.BlockSpec((groups, pl.squeezed, tok, width), lambda n, i=i: (0, i, 0, 0))
            for i in range(3)
        ],
        out_specs=[
            pl.BlockSpec((groups, tok, width), lambda n: (0, 0, 0)),
            pl.BlockSpec((heads, 1, length), lambda n: (0, 0, 0)),
        ],
        compiler_params=params(32),
        cost_estimate=cost(4 * heads * length * length * HEAD, 8 * length * width, heads * length * length),
        name="attend",
    )(qkv, qkv, qkv)


def attend_back(qkv, lse, grad):
    groups, _, tok, width = qkv.shape
    heads, length = width // HEAD, groups * tok
    rows = 256

    def body(q_ref, k_ref, v_ref, lse_ref, g_ref, dq_ref, dk_ref, dv_ref, k_acc, v_acc):
        keys = k_ref[...].reshape(length, HEAD)
        values = v_ref[...].reshape(length, HEAD)
        for b in range(length // rows):
            per = rows // tok
            query = q_ref[b * per : (b + 1) * per].reshape(rows, HEAD)
            grad_rows = g_ref[b * per : (b + 1) * per].reshape(rows, HEAD)
            scores = nt(keys, query) * (SCALE * LOG2E)
            probs = jnp.exp2(scores - lse_ref[:, b * rows : (b + 1) * rows])
            grad_probs = nt(values, grad_rows)
            delta = jnp.sum(probs * grad_probs, axis=0, keepdims=True)
            grad_scores = (probs * (grad_probs - delta)).astype(jnp.bfloat16)
            dv = jnp.dot(probs.astype(jnp.bfloat16), grad_rows, preferred_element_type=jnp.float32)
            dk = jnp.dot(grad_scores, query, preferred_element_type=jnp.float32)
            if b == 0:
                v_acc[...] = dv
                k_acc[...] = dk
            else:
                v_acc[...] += dv
                k_acc[...] += dk
            dq = tn(keys, grad_scores) * SCALE
            dq_ref[b * rows : (b + 1) * rows, :] = dq.T.astype(jnp.bfloat16)
        dk_ref[...] = (k_acc[...] * SCALE).astype(jnp.bfloat16)
        dv_ref[...] = v_acc[...].astype(jnp.bfloat16)

    out = jax.ShapeDtypeStruct((length, width), jnp.bfloat16)
    return pl.pallas_call(
        body,
        grid=(heads,),
        out_shape=[out] * 3,
        in_specs=[head_spec(groups, tok, i) for i in range(3)]
        + [
            pl.BlockSpec((pl.squeezed, 1, length), lambda h: (h, 0, 0)),
            pl.BlockSpec((groups, tok, HEAD), lambda h: (0, 0, h)),
        ],
        out_specs=[pl.BlockSpec((length, HEAD), lambda h: (0, h))] * 3,
        scratch_shapes=[pltpu.VMEM((length, HEAD), jnp.float32)] * 2,
        compiler_params=params(40),
        cost_estimate=cost(20 * heads * length * length * HEAD, 14 * length * width, heads * length * length),
        name="attend_back",
    )(qkv, qkv, qkv, lse, grad)


def grad_attended_parts(grads, weights):
    rows, width = grads.shape
    tok = rows // X
    _, feat, block = weights.shape
    groups = feat // BLOCK

    def body(g_ref, w_ref, *outs):
        total = None
        for j in range(4):
            term = nt(g_ref[:, j * block : (j + 1) * block], w_ref[j])
            total = term if total is None else total + term
        total = total.astype(jnp.bfloat16)
        for s in range(X):
            outs[s][...] = total[s * tok : (s + 1) * tok]

    return pl.pallas_call(
        body,
        grid=(groups,),
        out_shape=[jax.ShapeDtypeStruct((groups, tok, BLOCK), jnp.bfloat16)] * X,
        in_specs=[
            pl.BlockSpec((rows, width), lambda n: (0, 0)),
            pl.BlockSpec((4, BLOCK, block), lambda n: (0, n, 0)),
        ],
        out_specs=[pl.BlockSpec((pl.squeezed, tok, BLOCK), lambda n: (n, 0, 0))] * X,
        compiler_params=params(32),
        cost_estimate=cost(2 * rows * width * feat, 2 * feat * width + 4 * rows * width),
        name="grad_attended",
    )(grads, weights)


def weight_parts(attended, grads, core, other=None):
    groups, tok, block = attended[0].shape
    rows, step = X * tok, 4

    extra = [] if other is None else [other]

    def body(*refs):
        a_refs, g_ref, out, cols = refs[:X], refs[X], refs[-2], refs[-1]

        @pl.when(pl.program_id(0) == 0)
        def _():
            for i in range(2):
                j = 2 * i + core
                cols[:, i * block : (i + 1) * block] = g_ref[:, j * block : (j + 1) * block]

        left = jnp.concatenate(
            [jnp.concatenate([a[i] for i in range(step)], axis=1) for a in a_refs], axis=0
        )
        piece = tn(left, cols[...])
        yl = lax.axis_index("yl")
        for g in range(step):
            for i in range(2):
                part = piece[g * block : (g + 1) * block, i * block : (i + 1) * block]
                at = yl + i - 2 * yl * i
                if other is not None:
                    part = part + refs[X + 1][at, g].astype(jnp.float32)
                out[at, g] = part.astype(jnp.bfloat16)

    return pl.pallas_call(
        body,
        grid=(groups // step,),
        out_shape=jax.ShapeDtypeStruct((2, groups, block, block), jnp.bfloat16),
        in_specs=[pl.BlockSpec((step, tok, block), lambda n: (n, 0, 0))] * X
        + [pl.BlockSpec(grads.shape, lambda n: (0, 0))]
        + [pl.BlockSpec((2, step, block, block), lambda n: (0, n, 0, 0))] * len(extra),
        out_specs=pl.BlockSpec((2, step, block, block), lambda n: (0, n, 0, 0)),
        scratch_shapes=[pltpu.VMEM((rows, 2 * block), jnp.bfloat16)],
        compiler_params=params(32),
        cost_estimate=cost(4 * rows * groups * block * block, 5 * MIB),
        name="weight_parts",
    )(*attended, grads, *extra)


def project(attended, weights):
    groups, tok, block = attended[0].shape
    rows, feat = X * tok, groups * block

    def body(*refs):
        a_refs, w_ref, outs, left = refs[:X], refs[X], refs[X + 1 : 2 * X + 1], refs[2 * X + 1]

        @pl.when(pl.program_id(0) == 0)
        def _():
            for s in range(X):
                for n in range(groups):
                    left[s * tok : (s + 1) * tok, n * block : (n + 1) * block] = a_refs[s][n]

        out = jnp.dot(left[...], w_ref[...], preferred_element_type=jnp.float32)
        out = out.astype(jnp.bfloat16)
        for s in range(X):
            outs[s][...] = out[s * tok : (s + 1) * tok]

    return pl.pallas_call(
        body,
        grid=(4,),
        out_shape=[jax.ShapeDtypeStruct((tok, 4 * block), jnp.bfloat16)] * X,
        in_specs=[pl.BlockSpec((groups, tok, block), lambda j: (0, 0, 0))] * X
        + [pl.BlockSpec((pl.squeezed, feat, block), lambda j: (j, 0, 0))],
        out_specs=[pl.BlockSpec((tok, block), lambda j: (0, j))] * X,
        scratch_shapes=[pltpu.VMEM((rows, feat), jnp.bfloat16)],
        compiler_params=params(24),
        cost_estimate=cost(8 * rows * feat * block, 7 * MIB),
        name="project",
    )(*attended, weights)


def shift_x(array, shift):
    return lax.ppermute(array, "x", [(i, (i + shift) % X) for i in range(X)])


def swap(array, axis):
    return lax.ppermute(array, axis, [(0, 1), (1, 0)])


def exchange(array, axes=SEQ):
    return lax.all_to_all(array, axes, 0, 0, tiled=False)


def after(arrays, *others):
    return lax.optimization_barrier((arrays, others))[0]


def f32_sum(*arrays):
    total = arrays[0].astype(jnp.float32)
    for array in arrays[1:]:
        total = total + array.astype(jnp.float32)
    return total


def shards(query_input, key_input, value_input, out_weight, grad_out):
    cols = grad_out.shape[2]
    half = out_weight.shape[0] // 2

    lower = swap(out_weight[:half], "yl")
    upper = lax.ppermute(out_weight[half:], ("yl", "yh"), [(i, 3 - i) for i in range(4)])
    packed = pack_qkv(query_input[0], key_input[0], value_input[0])
    qkv = exchange(after(packed, lower, upper))
    mine = pack_grad(after(grad_out, packed)[0])
    grads = [mine[0]] + [shift_x(mine[s], s) for s in range(1, X)]
    grads = jnp.concatenate(grads, axis=0)
    weights = [out_weight, swap(out_weight, "core")]
    weights.append(jnp.concatenate([lower, upper], axis=0))
    weights.append(jnp.concatenate([swap(lower, "core"), swap(upper, "core")], axis=0))
    weights = jnp.stack(weights)
    parts = grad_attended_parts(grads, weights)

    attended, lse = attend(after(qkv, *parts))
    parts = [parts[0]] + [shift_x(parts[s], -s) for s in range(1, X)]
    attended = after(exchange(attended), *parts)
    rows = [attended] + [shift_x(attended, s) for s in range(1, X)]
    grad_attended = exchange(f32_sum(*parts).astype(jnp.bfloat16))

    grads = after(grads, grad_attended)
    far = swap(weight_parts(rows, grads, 1), "core")
    total = weight_parts(rows, grads, 0, far)
    total = exchange(total.reshape(-1, BLOCK, BLOCK), ("yl", *SEQ))
    grad_weight = jnp.sum(total.astype(jnp.float32), axis=0)

    grads_in = attend_back(qkv, lse, grad_attended)
    projected = project(rows, after(weights, grads_in[0]))
    projected = [projected[0]] + [shift_x(projected[s], -s) for s in range(1, X)]
    projected = place_projected(projected, cols)[None]

    return (projected, *[g[None] for g in grads_in], grad_weight)


def solution(mesh):
    fine = Mesh(mesh.devices.reshape(-1, X, 2, X, 2), DP + SEQ)
    return jax.shard_map(
        shards,
        mesh=fine,
        in_specs=(P(DP, SEQ, None), P(DP, SEQ, None), P(DP, SEQ, None), P(None, DP), P(DP, SEQ, None)),
        out_specs=(P(DP, SEQ, None), P(DP, None, SEQ), P(DP, None, SEQ), P(DP, None, SEQ), P(SEQ, DP)),
        check_vma=False,
    )
```

```python
import jax
import jax.numpy as jnp
from jax import lax
from jax.experimental import pallas as pl
from jax.experimental.pallas import tpu as pltpu
from jax.sharding import Mesh
from jax.sharding import PartitionSpec as P

HEAD = 128
X = 4
DP = ("yl", "x", "core")
SEQ = ("z", "yh")
BLOCK = 256
SCALE = HEAD ** (-0.5)
LOG2E = 1.4426950408889634
MIB = 1 << 20


def params(mib):
    return pltpu.CompilerParams(vmem_limit_bytes=mib * MIB)


def cost(flops, size, trans=0):
    return pl.CostEstimate(flops=flops, bytes_accessed=size, transcendentals=trans)


def nt(a, b):
    return lax.dot_general(a, b, (((1,), (1,)), ((), ())), preferred_element_type=jnp.float32)


def tn(a, b):
    return lax.dot_general(a, b, (((0,), (0,)), ((), ())), preferred_element_type=jnp.float32)


def place():
    return tuple(lax.axis_index(name) for name in DP)


def column_of(yl, x, core, j):
    other_y, other_core = j // 2, j % 2
    yy = yl + other_y - 2 * yl * other_y
    cc = core + other_core - 2 * core * other_core
    return pl.multiple_of(((yy * X + x) * 2 + cc) * BLOCK, BLOCK)


def pack_qkv(query, key, value):
    tok, feat = query.shape
    groups = feat // BLOCK

    def body(q, k, v, out):
        for g in range(groups):
            for i, src in enumerate((q, k, v)):
                out[g, i] = src[:, g * BLOCK : (g + 1) * BLOCK]

    return pl.pallas_call(
        body,
        out_shape=jax.ShapeDtypeStruct((groups, 3, tok, BLOCK), query.dtype),
        compiler_params=params(8),
        cost_estimate=cost(0, 3 * 2 * 2 * tok * feat),
        name="pack_qkv",
    )(query, key, value)


def pack_grad(grad):
    tok, cols = grad.shape

    def body(src, *outs):
        yl, x, core = place()
        for s in range(X):
            for j in range(4):
                outs[s][:, j * BLOCK : (j + 1) * BLOCK] = src[
                    :, pl.ds(column_of(yl, (x + s) % X, core, j), BLOCK)
                ]

    return pl.pallas_call(
        body,
        out_shape=[jax.ShapeDtypeStruct((tok, 4 * BLOCK), grad.dtype)] * X,
        compiler_params=params(6),
        cost_estimate=cost(0, 4 * tok * cols),
        name="pack_grad",
    )(grad)


def place_projected(parts, cols):
    tok = parts[0].shape[0]

    def body(*refs):
        srcs, out = refs[:X], refs[X]
        yl, x, core = place()
        for s in range(X):
            for j in range(4):
                out[:, pl.ds(column_of(yl, (x + s) % X, core, j), BLOCK)] = srcs[s][
                    :, j * BLOCK : (j + 1) * BLOCK
                ]

    return pl.pallas_call(
        body,
        out_shape=jax.ShapeDtypeStruct((tok, cols), parts[0].dtype),
        compiler_params=params(6),
        cost_estimate=cost(0, 4 * tok * cols),
        name="place_projected",
    )(*parts)


def head_spec(groups, tok, i):
    return pl.BlockSpec((groups, pl.squeezed, tok, HEAD), lambda h: (0, i, 0, h))


def attend(qkv):
    groups, _, tok, width = qkv.shape
    heads, length = width // HEAD, groups * tok

    def body(q_ref, k_ref, v_ref, o_ref, lse_ref):
        for h in range(heads):
            cols = slice(h * HEAD, (h + 1) * HEAD)
            keys = k_ref[:, :, cols].reshape(length, HEAD)
            values = v_ref[:, :, cols].reshape(length, HEAD)
            for b in range(groups):
                scores = nt(keys, q_ref[b, :, cols]) * (SCALE * LOG2E)
                peak = jnp.max(scores, axis=0, keepdims=True)
                shifted = jnp.exp2(scores - peak)
                total = jnp.sum(shifted, axis=0, keepdims=True)
                out = tn(values, shifted.astype(jnp.bfloat16)) / total
                o_ref[b, :, cols] = out.T.astype(jnp.bfloat16)
                lse_ref[h, :, b * tok : (b + 1) * tok] = peak + jnp.log2(total)

    return pl.pallas_call(
        body,
        grid=(1,),
        out_shape=[
            jax.ShapeDtypeStruct((groups, tok, width), jnp.bfloat16),
            jax.ShapeDtypeStruct((heads, 1, length), jnp.float32),
        ],
        in_specs=[
            pl.BlockSpec((groups, pl.squeezed, tok, width), lambda n, i=i: (0, i, 0, 0))
            for i in range(3)
        ],
        out_specs=[
            pl.BlockSpec((groups, tok, width), lambda n: (0, 0, 0)),
            pl.BlockSpec((heads, 1, length), lambda n: (0, 0, 0)),
        ],
        compiler_params=params(14),
        cost_estimate=cost(4 * heads * length * length * HEAD, 8 * length * width, heads * length * length),
        name="attend",
    )(qkv, qkv, qkv)


def attend_back(qkv, lse, grad):
    groups, _, tok, width = qkv.shape
    heads, length = width // HEAD, groups * tok
    rows = 256

    def body(q_ref, k_ref, v_ref, lse_ref, g_ref, dq_ref, dk_ref, dv_ref, k_acc, v_acc):
        keys = k_ref[...].reshape(length, HEAD)
        values = v_ref[...].reshape(length, HEAD)
        for b in range(length // rows):
            per = rows // tok
            query = q_ref[b * per : (b + 1) * per].reshape(rows, HEAD)
            grad_rows = g_ref[b * per : (b + 1) * per].reshape(rows, HEAD)
            scores = nt(keys, query) * (SCALE * LOG2E)
            probs = jnp.exp2(scores - lse_ref[:, b * rows : (b + 1) * rows])
            grad_probs = nt(values, grad_rows)
            delta = jnp.sum(probs * grad_probs, axis=0, keepdims=True)
            grad_scores = (probs * (grad_probs - delta)).astype(jnp.bfloat16)
            dv = jnp.dot(probs.astype(jnp.bfloat16), grad_rows, preferred_element_type=jnp.float32)
            dk = jnp.dot(grad_scores, query, preferred_element_type=jnp.float32)
            if b == 0:
                v_acc[...] = dv
                k_acc[...] = dk
            else:
                v_acc[...] += dv
                k_acc[...] += dk
            dq = tn(keys, grad_scores) * SCALE
            dq_ref[b * rows : (b + 1) * rows, :] = dq.T.astype(jnp.bfloat16)
        dk_ref[...] = (k_acc[...] * SCALE).astype(jnp.bfloat16)
        dv_ref[...] = v_acc[...].astype(jnp.bfloat16)

    out = jax.ShapeDtypeStruct((length, width), jnp.bfloat16)
    return pl.pallas_call(
        body,
        grid=(heads,),
        out_shape=[out] * 3,
        in_specs=[head_spec(groups, tok, i) for i in range(3)]
        + [
            pl.BlockSpec((pl.squeezed, 1, length), lambda h: (h, 0, 0)),
            pl.BlockSpec((groups, tok, HEAD), lambda h: (0, 0, h)),
        ],
        out_specs=[pl.BlockSpec((length, HEAD), lambda h: (0, h))] * 3,
        scratch_shapes=[pltpu.VMEM((length, HEAD), jnp.float32)] * 2,
        compiler_params=params(22),
        cost_estimate=cost(20 * heads * length * length * HEAD, 14 * length * width, heads * length * length),
        name="attend_back",
    )(qkv, qkv, qkv, lse, grad)


def grad_attended_parts(grads, weights):
    rows, width = grads.shape
    tok = rows // X
    _, feat, block = weights.shape
    groups = feat // BLOCK

    def body(g_ref, w_ref, *outs):
        total = None
        for j in range(4):
            term = nt(g_ref[:, j * block : (j + 1) * block], w_ref[j])
            total = term if total is None else total + term
        total = total.astype(jnp.bfloat16)
        for s in range(X):
            outs[s][...] = total[s * tok : (s + 1) * tok]

    return pl.pallas_call(
        body,
        grid=(groups,),
        out_shape=[jax.ShapeDtypeStruct((groups, tok, BLOCK), jnp.bfloat16)] * X,
        in_specs=[
            pl.BlockSpec((rows, width), lambda n: (0, 0)),
            pl.BlockSpec((4, BLOCK, block), lambda n: (0, n, 0)),
        ],
        out_specs=[pl.BlockSpec((pl.squeezed, tok, BLOCK), lambda n: (n, 0, 0))] * X,
        compiler_params=params(12),
        cost_estimate=cost(2 * rows * width * feat, 2 * feat * width + 4 * rows * width),
        name="grad_attended",
    )(grads, weights)


def weight_parts(attended, grads, core, other=None):
    groups, tok, block = attended[0].shape
    rows, step = X * tok, 4

    extra = [] if other is None else [other]

    def body(*refs):
        a_refs, g_ref, out, cols = refs[:X], refs[X], refs[-2], refs[-1]

        @pl.when(pl.program_id(0) == 0)
        def _():
            for i in range(2):
                j = 2 * i + core
                cols[:, i * block : (i + 1) * block] = g_ref[:, j * block : (j + 1) * block]

        left = jnp.concatenate(
            [jnp.concatenate([a[i] for i in range(step)], axis=1) for a in a_refs], axis=0
        )
        piece = tn(left, cols[...])
        yl = lax.axis_index("yl")
        for g in range(step):
            for i in range(2):
                part = piece[g * block : (g + 1) * block, i * block : (i + 1) * block]
                at = yl + i - 2 * yl * i
                if other is not None:
                    part = part + refs[X + 1][at, g].astype(jnp.float32)
                out[at, g] = part.astype(jnp.bfloat16)

    return pl.pallas_call(
        body,
        grid=(groups // step,),
        out_shape=jax.ShapeDtypeStruct((2, groups, block, block), jnp.bfloat16),
        in_specs=[pl.BlockSpec((step, tok, block), lambda n: (n, 0, 0))] * X
        + [pl.BlockSpec(grads.shape, lambda n: (0, 0))]
        + [pl.BlockSpec((2, step, block, block), lambda n: (0, n, 0, 0))] * len(extra),
        out_specs=pl.BlockSpec((2, step, block, block), lambda n: (0, n, 0, 0)),
        scratch_shapes=[pltpu.VMEM((rows, 2 * block), jnp.bfloat16)],
        compiler_params=params(18),
        cost_estimate=cost(4 * rows * groups * block * block, 5 * MIB),
        name="weight_parts",
    )(*attended, grads, *extra)


def project(attended, weights):
    groups, tok, block = attended[0].shape
    rows, feat = X * tok, groups * block

    def body(*refs):
        a_refs, w_ref, outs, left = refs[:X], refs[X], refs[X + 1 : 2 * X + 1], refs[2 * X + 1]

        @pl.when(pl.program_id(0) == 0)
        def _():
            for s in range(X):
                for n in range(groups):
                    left[s * tok : (s + 1) * tok, n * block : (n + 1) * block] = a_refs[s][n]

        out = jnp.dot(left[...], w_ref[...], preferred_element_type=jnp.float32)
        out = out.astype(jnp.bfloat16)
        for s in range(X):
            outs[s][...] = out[s * tok : (s + 1) * tok]

    return pl.pallas_call(
        body,
        grid=(4,),
        out_shape=[jax.ShapeDtypeStruct((tok, 4 * block), jnp.bfloat16)] * X,
        in_specs=[pl.BlockSpec((groups, tok, block), lambda j: (0, 0, 0))] * X
        + [pl.BlockSpec((pl.squeezed, feat, block), lambda j: (j, 0, 0))],
        out_specs=[pl.BlockSpec((tok, block), lambda j: (0, j))] * X,
        scratch_shapes=[pltpu.VMEM((rows, feat), jnp.bfloat16)],
        compiler_params=params(16),
        cost_estimate=cost(8 * rows * feat * block, 7 * MIB),
        name="project",
    )(*attended, weights)


def shift_x(array, shift):
    return lax.ppermute(array, "x", [(i, (i + shift) % X) for i in range(X)])


def swap(array, axis):
    return lax.ppermute(array, axis, [(0, 1), (1, 0)])


def exchange(array, axes=SEQ):
    return lax.all_to_all(array, axes, 0, 0, tiled=False)


def after(arrays, *others):
    return lax.optimization_barrier((arrays, others))[0]


def f32_sum(*arrays):
    total = arrays[0].astype(jnp.float32)
    for array in arrays[1:]:
        total = total + array.astype(jnp.float32)
    return total


def shards(query_input, key_input, value_input, out_weight, grad_out):
    cols = grad_out.shape[2]
    half = out_weight.shape[0] // 2

    lower = swap(out_weight[:half], "yl")
    upper = lax.ppermute(out_weight[half:], ("yl", "yh"), [(i, 3 - i) for i in range(4)])
    packed = pack_qkv(query_input[0], key_input[0], value_input[0])
    qkv = exchange(after(packed, lower, upper))
    mine = pack_grad(after(grad_out, packed)[0])
    grads = [mine[0]] + [shift_x(mine[s], s) for s in range(1, X)]
    grads = jnp.concatenate(grads, axis=0)
    weights = [out_weight, swap(out_weight, "core")]
    weights.append(jnp.concatenate([lower, upper], axis=0))
    weights.append(jnp.concatenate([swap(lower, "core"), swap(upper, "core")], axis=0))
    weights = jnp.stack(weights)
    parts = grad_attended_parts(grads, weights)

    attended, lse = attend(after(qkv, *parts))
    parts = [parts[0]] + [shift_x(parts[s], -s) for s in range(1, X)]
    attended = after(exchange(attended), *parts)
    rows = [attended] + [shift_x(attended, s) for s in range(1, X)]
    grad_attended = exchange(f32_sum(*parts).astype(jnp.bfloat16))

    grads = after(grads, grad_attended)
    far = swap(weight_parts(rows, grads, 1), "core")
    total = weight_parts(rows, grads, 0, far)
    total = exchange(total.reshape(-1, BLOCK, BLOCK), ("yl", *SEQ))
    grad_weight = jnp.sum(total.astype(jnp.float32), axis=0)

    grads_in = attend_back(qkv, lse, grad_attended)
    projected = project(rows, after(weights, grads_in[0]))
    projected = [projected[0]] + [shift_x(projected[s], -s) for s in range(1, X)]
    projected = place_projected(projected, cols)[None]

    return (projected, *[g[None] for g in grads_in], grad_weight)


def solution(mesh):
    fine = Mesh(mesh.devices.reshape(-1, X, 2, X, 2), DP + SEQ)
    return jax.shard_map(
        shards,
        mesh=fine,
        in_specs=(P(DP, SEQ, None), P(DP, SEQ, None), P(DP, SEQ, None), P(None, DP), P(DP, SEQ, None)),
        out_specs=(P(DP, SEQ, None), P(DP, None, SEQ), P(DP, None, SEQ), P(DP, None, SEQ), P(SEQ, DP)),
        check_vma=False,
    )
```

```python
import jax
import jax.numpy as jnp
from jax import lax
from jax.experimental import pallas as pl
from jax.experimental.pallas import tpu as pltpu
from jax.sharding import Mesh
from jax.sharding import PartitionSpec as P

HEAD = 128
X = 4
DP = ("yl", "x", "core")
SEQ = ("z", "yh")
BLOCK = 256
SCALE = HEAD ** (-0.5)
LOG2E = 1.4426950408889634
MIB = 1 << 20


def params(mib):
    return pltpu.CompilerParams(vmem_limit_bytes=mib * MIB)


def cost(flops, size, trans=0):
    return pl.CostEstimate(flops=flops, bytes_accessed=size, transcendentals=trans)


def nt(a, b):
    return lax.dot_general(a, b, (((1,), (1,)), ((), ())), preferred_element_type=jnp.float32)


def tn(a, b):
    return lax.dot_general(a, b, (((0,), (0,)), ((), ())), preferred_element_type=jnp.float32)


def place():
    return tuple(lax.axis_index(name) for name in DP)


def column_of(yl, x, core, j):
    other_y, other_core = j // 2, j % 2
    yy = yl + other_y - 2 * yl * other_y
    cc = core + other_core - 2 * core * other_core
    return pl.multiple_of(((yy * X + x) * 2 + cc) * BLOCK, BLOCK)


def pack_qkv(query, key, value):
    tok, feat = query.shape
    groups = feat // BLOCK

    def body(q, k, v, out):
        for g in range(groups):
            for i, src in enumerate((q, k, v)):
                out[g, i] = src[:, g * BLOCK : (g + 1) * BLOCK]

    return pl.pallas_call(
        body,
        out_shape=jax.ShapeDtypeStruct((groups, 3, tok, BLOCK), query.dtype),
        compiler_params=params(8),
        cost_estimate=cost(0, 3 * 2 * 2 * tok * feat),
        name="pack_qkv",
    )(query, key, value)


def pack_grad(grad):
    tok, cols = grad.shape

    def body(src, *outs):
        yl, x, core = place()
        for s in range(X):
            for j in range(4):
                outs[s][:, j * BLOCK : (j + 1) * BLOCK] = src[
                    :, pl.ds(column_of(yl, (x + s) % X, core, j), BLOCK)
                ]

    return pl.pallas_call(
        body,
        out_shape=[jax.ShapeDtypeStruct((tok, 4 * BLOCK), grad.dtype)] * X,
        compiler_params=params(6),
        cost_estimate=cost(0, 4 * tok * cols),
        name="pack_grad",
    )(grad)


def place_projected(parts, cols):
    tok = parts[0].shape[0]

    def body(*refs):
        srcs, out = refs[:X], refs[X]
        yl, x, core = place()
        for s in range(X):
            for j in range(4):
                out[:, pl.ds(column_of(yl, (x + s) % X, core, j), BLOCK)] = srcs[s][
                    :, j * BLOCK : (j + 1) * BLOCK
                ]

    return pl.pallas_call(
        body,
        out_shape=jax.ShapeDtypeStruct((tok, cols), parts[0].dtype),
        compiler_params=params(6),
        cost_estimate=cost(0, 4 * tok * cols),
        name="place_projected",
    )(*parts)


def head_spec(groups, tok, i):
    return pl.BlockSpec((groups, pl.squeezed, tok, HEAD), lambda h: (0, i, 0, h))


def attend(qkv):
    groups, _, tok, width = qkv.shape
    heads, length = width // HEAD, groups * tok

    def body(q_ref, k_ref, v_ref, o_ref, lse_ref):
        for h in range(heads):
            cols = slice(h * HEAD, (h + 1) * HEAD)
            keys = k_ref[:, :, cols].reshape(length, HEAD)
            values = v_ref[:, :, cols].reshape(length, HEAD)
            for b in range(groups):
                scores = nt(keys, q_ref[b, :, cols]) * (SCALE * LOG2E)
                peak = jnp.max(scores, axis=0, keepdims=True)
                shifted = jnp.exp2(scores - peak)
                total = jnp.sum(shifted, axis=0, keepdims=True)
                out = tn(values, shifted.astype(jnp.bfloat16)) / total
                o_ref[b, :, cols] = out.T.astype(jnp.bfloat16)
                lse_ref[h, :, b * tok : (b + 1) * tok] = peak + jnp.log2(total)

    return pl.pallas_call(
        body,
        grid=(1,),
        out_shape=[
            jax.ShapeDtypeStruct((groups, tok, width), jnp.bfloat16),
            jax.ShapeDtypeStruct((heads, 1, length), jnp.float32),
        ],
        in_specs=[
            pl.BlockSpec((groups, pl.squeezed, tok, width), lambda n, i=i: (0, i, 0, 0))
            for i in range(3)
        ],
        out_specs=[
            pl.BlockSpec((groups, tok, width), lambda n: (0, 0, 0)),
            pl.BlockSpec((heads, 1, length), lambda n: (0, 0, 0)),
        ],
        compiler_params=params(14),
        cost_estimate=cost(4 * heads * length * length * HEAD, 8 * length * width, heads * length * length),
        name="attend",
    )(qkv, qkv, qkv)


def attend_back(qkv, lse, grad):
    groups, _, tok, width = qkv.shape
    heads, length = width // HEAD, groups * tok
    rows = 256

    def body(q_ref, k_ref, v_ref, lse_ref, g_ref, dq_ref, dk_ref, dv_ref, k_acc, v_acc):
        keys = k_ref[...].reshape(length, HEAD)
        values = v_ref[...].reshape(length, HEAD)
        for b in range(length // rows):
            per = rows // tok
            query = q_ref[b * per : (b + 1) * per].reshape(rows, HEAD)
            grad_rows = g_ref[b * per : (b + 1) * per].reshape(rows, HEAD)
            scores = nt(keys, query) * (SCALE * LOG2E)
            probs = jnp.exp2(scores - lse_ref[:, b * rows : (b + 1) * rows])
            grad_probs = nt(values, grad_rows)
            delta = jnp.sum(probs * grad_probs, axis=0, keepdims=True)
            grad_scores = (probs * (grad_probs - delta)).astype(jnp.bfloat16)
            dv = jnp.dot(probs.astype(jnp.bfloat16), grad_rows, preferred_element_type=jnp.float32)
            dk = jnp.dot(grad_scores, query, preferred_element_type=jnp.float32)
            if b == 0:
                v_acc[...] = dv
                k_acc[...] = dk
            else:
                v_acc[...] += dv
                k_acc[...] += dk
            dq = tn(keys, grad_scores) * SCALE
            dq_ref[b * rows : (b + 1) * rows, :] = dq.T.astype(jnp.bfloat16)
        dk_ref[...] = (k_acc[...] * SCALE).astype(jnp.bfloat16)
        dv_ref[...] = v_acc[...].astype(jnp.bfloat16)

    out = jax.ShapeDtypeStruct((length, width), jnp.bfloat16)
    return pl.pallas_call(
        body,
        grid=(heads,),
        out_shape=[out] * 3,
        in_specs=[head_spec(groups, tok, i) for i in range(3)]
        + [
            pl.BlockSpec((pl.squeezed, 1, length), lambda h: (h, 0, 0)),
            pl.BlockSpec((groups, tok, HEAD), lambda h: (0, 0, h)),
        ],
        out_specs=[pl.BlockSpec((length, HEAD), lambda h: (0, h))] * 3,
        scratch_shapes=[pltpu.VMEM((length, HEAD), jnp.float32)] * 2,
        compiler_params=params(22),
        cost_estimate=cost(20 * heads * length * length * HEAD, 14 * length * width, heads * length * length),
        name="attend_back",
    )(qkv, qkv, qkv, lse, grad)


def grad_attended_parts(grads, weights):
    rows, width = grads.shape
    tok = rows // X
    _, feat, block = weights.shape
    groups = feat // BLOCK

    def body(g_ref, w_ref, *outs):
        total = None
        for j in range(4):
            term = nt(g_ref[:, j * block : (j + 1) * block], w_ref[j])
            total = term if total is None else total + term
        total = total.astype(jnp.bfloat16)
        for s in range(X):
            outs[s][...] = total[s * tok : (s + 1) * tok]

    return pl.pallas_call(
        body,
        grid=(groups,),
        out_shape=[jax.ShapeDtypeStruct((groups, tok, BLOCK), jnp.bfloat16)] * X,
        in_specs=[
            pl.BlockSpec((rows, width), lambda n: (0, 0)),
            pl.BlockSpec((4, BLOCK, block), lambda n: (0, n, 0)),
        ],
        out_specs=[pl.BlockSpec((pl.squeezed, tok, BLOCK), lambda n: (n, 0, 0))] * X,
        compiler_params=params(12),
        cost_estimate=cost(2 * rows * width * feat, 2 * feat * width + 4 * rows * width),
        name="grad_attended",
    )(grads, weights)


def weight_parts(attended, grads, core, other=None):
    groups, tok, block = attended[0].shape
    rows, step = X * tok, 4

    extra = [] if other is None else [other]

    def body(*refs):
        a_refs, g_ref, out, cols = refs[:X], refs[X], refs[-2], refs[-1]

        @pl.when(pl.program_id(0) == 0)
        def _():
            for i in range(2):
                j = 2 * i + core
                cols[:, i * block : (i + 1) * block] = g_ref[:, j * block : (j + 1) * block]

        left = jnp.concatenate(
            [jnp.concatenate([a[i] for i in range(step)], axis=1) for a in a_refs], axis=0
        )
        piece = tn(left, cols[...])
        yl = lax.axis_index("yl")
        for g in range(step):
            for i in range(2):
                part = piece[g * block : (g + 1) * block, i * block : (i + 1) * block]
                at = yl + i - 2 * yl * i
                if other is not None:
                    part = part + refs[X + 1][at, g].astype(jnp.float32)
                out[at, g] = part.astype(jnp.bfloat16)

    return pl.pallas_call(
        body,
        grid=(groups // step,),
        out_shape=jax.ShapeDtypeStruct((2, groups, block, block), jnp.bfloat16),
        in_specs=[pl.BlockSpec((step, tok, block), lambda n: (n, 0, 0))] * X
        + [pl.BlockSpec(grads.shape, lambda n: (0, 0))]
        + [pl.BlockSpec((2, step, block, block), lambda n: (0, n, 0, 0))] * len(extra),
        out_specs=pl.BlockSpec((2, step, block, block), lambda n: (0, n, 0, 0)),
        scratch_shapes=[pltpu.VMEM((rows, 2 * block), jnp.bfloat16)],
        compiler_params=params(18),
        cost_estimate=cost(4 * rows * groups * block * block, 5 * MIB),
        name="weight_parts",
    )(*attended, grads, *extra)


def project(attended, weights):
    groups, tok, block = attended[0].shape
    rows, feat = X * tok, groups * block

    def body(*refs):
        a_refs, w_ref, outs, left = refs[:X], refs[X], refs[X + 1 : 2 * X + 1], refs[2 * X + 1]

        @pl.when(pl.program_id(0) == 0)
        def _():
            for s in range(X):
                for n in range(groups):
                    left[s * tok : (s + 1) * tok, n * block : (n + 1) * block] = a_refs[s][n]

        out = jnp.dot(left[...], w_ref[...], preferred_element_type=jnp.float32)
        out = out.astype(jnp.bfloat16)
        for s in range(X):
            outs[s][...] = out[s * tok : (s + 1) * tok]

    return pl.pallas_call(
        body,
        grid=(4,),
        out_shape=[jax.ShapeDtypeStruct((tok, 4 * block), jnp.bfloat16)] * X,
        in_specs=[pl.BlockSpec((groups, tok, block), lambda j: (0, 0, 0))] * X
        + [pl.BlockSpec((pl.squeezed, feat, block), lambda j: (j, 0, 0))],
        out_specs=[pl.BlockSpec((tok, block), lambda j: (0, j))] * X,
        scratch_shapes=[pltpu.VMEM((rows, feat), jnp.bfloat16)],
        compiler_params=params(16),
        cost_estimate=cost(8 * rows * feat * block, 7 * MIB),
        name="project",
    )(*attended, weights)


def shift_x(array, shift):
    return lax.ppermute(array, "x", [(i, (i + shift) % X) for i in range(X)])


def swap(array, axis):
    return lax.ppermute(array, axis, [(0, 1), (1, 0)])


def exchange(array, axes=SEQ):
    return lax.all_to_all(array, axes, 0, 0, tiled=False)


def after(arrays, *others):
    return lax.optimization_barrier((arrays, others))[0]


def f32_sum(*arrays):
    total = arrays[0].astype(jnp.float32)
    for array in arrays[1:]:
        total = total + array.astype(jnp.float32)
    return total


def shards(query_input, key_input, value_input, out_weight, grad_out):
    cols = grad_out.shape[2]
    half = out_weight.shape[0] // 2

    lower = swap(out_weight[:half], "yl")
    upper = lax.ppermute(out_weight[half:], ("yl", "yh"), [(i, 3 - i) for i in range(4)])
    packed = pack_qkv(query_input[0], key_input[0], value_input[0])
    qkv = exchange(after(packed, lower, upper))
    mine = pack_grad(after(grad_out, packed)[0])
    grads = [mine[0]] + [shift_x(mine[s], s) for s in range(1, X)]
    grads = jnp.concatenate(grads, axis=0)
    weights = [out_weight, swap(out_weight, "core")]
    weights.append(jnp.concatenate([lower, upper], axis=0))
    weights.append(jnp.concatenate([swap(lower, "core"), swap(upper, "core")], axis=0))
    weights = jnp.stack(weights)
    parts = grad_attended_parts(grads, weights)

    attended, lse = attend(after(qkv, *parts))
    parts = [parts[0]] + [shift_x(parts[s], -s) for s in range(1, X)]
    attended = after(exchange(attended), *parts[1:3])
    rows = [attended] + [shift_x(attended, s) for s in range(1, X)]
    grad_attended = exchange(f32_sum(*parts).astype(jnp.bfloat16))

    grads = after(grads, grad_attended)
    far = swap(weight_parts(rows, grads, 1), "core")
    total = weight_parts(rows, grads, 0, far)
    total = exchange(total.reshape(-1, BLOCK, BLOCK), ("yl", *SEQ))
    grad_weight = jnp.sum(total.astype(jnp.float32), axis=0)

    grads_in = attend_back(qkv, lse, grad_attended)
    projected = project(rows, after(weights, grads_in[0]))
    projected = [projected[0]] + [shift_x(projected[s], -s) for s in range(1, X)]
    projected = place_projected(projected, cols)[None]

    return (projected, *[g[None] for g in grads_in], grad_weight)


def solution(mesh):
    fine = Mesh(mesh.devices.reshape(-1, X, 2, X, 2), DP + SEQ)
    return jax.shard_map(
        shards,
        mesh=fine,
        in_specs=(P(DP, SEQ, None), P(DP, SEQ, None), P(DP, SEQ, None), P(None, DP), P(DP, SEQ, None)),
        out_specs=(P(DP, SEQ, None), P(DP, None, SEQ), P(DP, None, SEQ), P(DP, None, SEQ), P(SEQ, DP)),
        check_vma=False,
    )
```
